32 devices in a mesh: ka: 4 (over x, core), rows: 8 (over z, y).
Axes of the slice: x: 2, y: 2, z: 4, core: 2. Of those that a mesh axis runs over, the one named last changes fastest.
Arguments:
- hoppings: bfloat16 [8, 384, 128, 128], P('rows', 'ka'), may hold values from -0.09375 to 0.09375
- tile_rows: int32 [8, 384], P('rows', 'ka'), may hold values from 0 to 95, as said below
- tile_cols: int32 [8, 384], P('rows', 'ka'), may hold values from 0 to 95, as said below
- tile_lats: int32 [8, 384], P('rows', 'ka'), may hold values from 0 to 8
- tile_counts: int32 [8, 4], P('rows', 'ka'), may hold values from 48 to 96, as said below
- phase_angle: float32 [8, 9], P('ka'), may hold values from -3.140625 to 3.140625
- vectors: bfloat16 [8, 2, 12288, 256], P('ka', None, 'rows'), may hold values from -6 to 6
Outputs:
- bloch_product: float32 [8, 2, 12288, 256], P('ka', None, 'rows')
The draws below stay inside these ranges and needn't reach their ends.
Inputs may be any that keep to these rules, and one draw needn't show every extreme that they name: `tile_rows`: slots of row block r (first index) hold tile rows r * 12 to (r + 1) * 12 - 1; several slots may name the same block. `tile_cols`: the cyclic distance between a slot's tile column and its tile row is at most 16, and both distances 16 occur in every row block. `tile_counts`: the live slots of a device are the first ones of its part of the list; some device has all 96 live.
All inputs are finite; a program needn't handle non-finite values.
Results may differ from the reference program's by a relative error of at most 0.0029.
Values may be sent and summed in bfloat16 or wider, within the bound.
A program may use at most 320 MiB of HBM per device.

```python
import jax
import jax.numpy as jnp
from jax import lax

TS = 128
TORB = 96
NLAT = 9
BAND = 16
NVEC = 256
TILE_DEV = 96
TR = 12
LISTS = 384
ORB = 12288
KPTS = 8
N_KA = 4
N_ROWS = 8


def tile_coordinates(key):
    folded_rows = jax.random.fold_in(key, 17)
    first_key, second_key = jax.random.split(folded_rows)
    row_position = jax.random.randint(first_key, (N_ROWS, TILE_DEV * N_KA), 0, TR)
    row_position = row_position + (jnp.arange(N_ROWS, dtype=jnp.int32) * TR)[:, None]
    column_step = jax.random.randint(second_key, (N_ROWS, TILE_DEV * N_KA), -BAND, BAND + 1)
    column_step = column_step.at[:, 0].set(BAND).at[:, 1].set(-BAND)
    col_index = jnp.mod(row_position + column_step, TORB)
    return (row_position.astype(jnp.int32), col_index.astype(jnp.int32))


def draw_tile_rows(key, part):
    return tile_coordinates(key)[0]


def draw_tile_cols(key, part):
    return tile_coordinates(key)[1]


def draw_tile_counts(key, part):
    folded_rows = jax.random.fold_in(key, 29)
    first_key, second_key = jax.random.split(folded_rows)
    counts = jax.random.randint(first_key, (N_ROWS * N_KA,), (TILE_DEV + 1) // 2, TILE_DEV + 1)
    full_slot = jax.random.randint(second_key, (), 0, N_ROWS * N_KA)
    counts = counts.at[full_slot].set(TILE_DEV)
    return counts.reshape(N_ROWS, N_KA).astype(jnp.int32)


def plant(result, rng, low, largest):
    longest = result.shape.index(max(result.shape))
    spots = []
    for shift in (0, 1):
        where = [jax.random.randint(jax.random.fold_in(rng, axis), (), 0, length) for axis, length in enumerate(result.shape)]
        where[longest] = (where[longest] + shift) % result.shape[longest]
        spots.append(tuple(where))
    return result.at[spots[0]].set(low).at[spots[1]].set(largest)


def shard_levels(key, extent, cuts, least, high):
    def one(dim, parts):
        steps = jax.random.uniform(jax.random.fold_in(jax.random.fold_in(key, 6), dim), (parts,), jnp.float32, least / len(cuts), high / len(cuts))
        return jnp.repeat(jnp.exp(steps), extent[dim] // parts).reshape((-1,) + (1,) * (len(extent) - dim - 1))

    factor_of = one(*cuts[0])
    for cut in cuts[1:]:
        factor_of = factor_of * one(*cut)
    return factor_of


def centred(rng, dims, spread, most, cuts=(), held_as=jnp.bfloat16):
    result = jax.random.normal(rng, dims, jnp.float32) * spread
    if len(cuts) > 0:
        result = shard_levels(rng, dims, cuts, -0.22, 0.18) * result
    return jnp.clip(result, min=-most, max=most).astype(held_as)


def setup_inputs(seed: int = 0) -> dict:
    streams_of = jax.random.split(jax.random.key(seed), 8)
    return {
        "hoppings": centred(streams_of[0], (N_ROWS, LISTS, TS, TS), (TS * TILE_DEV * N_KA // TR) ** -0.5, 0.09375, ((0, 8), (1, 4))),
        "tile_rows": draw_tile_rows(jax.random.fold_in(streams_of[7], 71), 0),
        "tile_cols": draw_tile_cols(jax.random.fold_in(streams_of[7], 71), 0),
        "tile_lats": plant(jax.random.randint(streams_of[3], (N_ROWS, LISTS), 0, NLAT), jax.random.fold_in(streams_of[3], 1), 0, NLAT - 1).astype(jnp.int32),
        "tile_counts": draw_tile_counts(jax.random.fold_in(streams_of[7], 71), 0),
        "phase_angle": jnp.clip(jax.random.uniform(streams_of[5], (KPTS, NLAT), jnp.float32, -3.140625, 3.140625), -3.140625, 3.140625),
        "vectors": centred(streams_of[6], (KPTS, 2, ORB, NVEC), 1.0, 6.0, ((0, 4), (2, 8))),
    }


def reference(hoppings, tile_rows, tile_cols, tile_lats, tile_counts, phase_angle, vectors):
    list_count = hoppings.shape[1]
    slot_index = jnp.arange(list_count, dtype=jnp.int32)
    live_mask = (slot_index[None, :] % TILE_DEV) < tile_counts[:, slot_index // TILE_DEV]
    live_f32 = live_mask.astype(jnp.float32)
    block_ids = (tile_rows * TORB + tile_cols).astype(jnp.int32)

    def one_point(point_data):
        angles, point_vectors = point_data
        cos_weight = jnp.cos(angles)[tile_lats] * live_f32
        sin_weight = jnp.sin(angles)[tile_lats] * live_f32

        def add_row_block(block, carry):
            real_acc, imag_acc = carry
            tile_block = lax.dynamic_index_in_dim(hoppings, block, 0, keepdims=False).astype(jnp.float32)
            destination_rows = lax.dynamic_index_in_dim(block_ids, block, 0, keepdims=False)
            cos_row = lax.dynamic_index_in_dim(cos_weight, block, 0, keepdims=False)
            sin_row = lax.dynamic_index_in_dim(sin_weight, block, 0, keepdims=False)
            real_acc = real_acc.at[destination_rows].add(cos_row[:, None, None] * tile_block)
            imag_acc = imag_acc.at[destination_rows].add(sin_row[:, None, None] * tile_block)
            return (real_acc, imag_acc)

        empty_blocks = jnp.zeros((TORB * TORB, TS, TS), jnp.float32)
        real_acc, imag_acc = lax.fori_loop(0, N_ROWS, add_row_block, (empty_blocks, empty_blocks))
        matrix = jnp.stack([real_acc, imag_acc]).astype(jnp.bfloat16)
        matrix = lax.optimization_barrier(matrix).astype(jnp.float32).reshape(2, TORB, TORB, TS, TS)
        vector_f32 = point_vectors.astype(jnp.float32).reshape(2, TORB, TS, NVEC)
        product = jnp.einsum('pijab,qjbv->piaqv', matrix, vector_f32, precision=lax.Precision.HIGHEST)
        real_part = product[0, :, :, 0] - product[1, :, :, 1]
        imag_part = product[0, :, :, 1] + product[1, :, :, 0]
        return jnp.stack([real_part, imag_part]).reshape(2, TORB * TS, NVEC)

    return lax.map(one_point, (phase_angle, vectors))
```

```python
import functools

import jax
import jax.numpy as jnp
from jax import lax
from jax.experimental import pallas as pl
from jax.experimental.pallas import tpu as pltpu
from jax.sharding import PartitionSpec as P

NLAT = 9
BAND = 16
GROUP = 4
DEPTH = 4
MESH = pl.DeviceIdType.MESH


def spans(total, size):
    return [(start, min(size, total - start)) for start in range(0, total, size)]


def exchange_kernel(group_size, row_shards, hop, meta, vec, all_hop, all_meta, win,
                    hop_own, meta_own, send_sem, recv_sem, local_sem):
    slots = hop.shape[0]
    row_tiles = vec.shape[2]
    ka = lax.axis_index("ka")
    row = lax.axis_index("rows")
    odd = lax.rem(row, 2)
    even = 1 - odd
    sign = 1 - 2 * odd
    partner = ka + 1 - 2 * lax.rem(ka, 2)
    reach = (BAND + row_tiles - 1) // row_tiles
    depth_of = lambda d: min(row_tiles, BAND - (d - 1) * row_tiles)

    def at_row(step):
        return {"ka": ka, "rows": lax.rem(row + step + 2 * row_shards, row_shards)}

    def at_ka(other):
        return {"ka": other, "rows": row}

    across = [lax.rem(ka + 2 * h, group_size) for h in range(1, group_size // 2)]
    others = [lax.rem(ka + h, group_size) for h in range(1, group_size)]
    forwarding = row_tiles <= BAND and row_shards % 2 == 0 and reach >= 2
    peers = [at_ka(o) for o in others]
    if forwarding:
        peers.append(at_row(sign))
    else:
        peers += [at_row(1), at_row(-1)]
    for d in range(2, reach + 1):
        peers += [at_row(d), at_row(-d)]

    barrier = pltpu.get_barrier_semaphore()
    for peer in peers:
        pl.semaphore_signal(barrier, inc=1, device_id=peer, device_id_type=MESH)

    fetch_hop = pltpu.make_async_copy(hop, hop_own, local_sem.at[0])
    fetch_meta = pltpu.make_async_copy(meta, meta_own, local_sem.at[1])
    fetch_hop.start()
    fetch_meta.start()
    pl.semaphore_wait(barrier, len(peers))

    made = []

    def send(src, dst, device):
        n = len(made)
        copy = pltpu.make_async_remote_copy(
            src_ref=src, dst_ref=dst, send_sem=send_sem.at[n], recv_sem=recv_sem.at[n],
            device_id=device, device_id_type=MESH)
        copy.start()
        made.append(copy)
        return copy

    received = set()

    def arrived(copy):
        copy.wait_recv()
        received.add(id(copy))

    def vec_send(tile, count, step):
        send_to = -step * row_tiles + tile + BAND
        return send(vec.at[:, :, pl.ds(tile, count)], win.at[:, :, pl.ds(send_to, count)], at_row(step))

    def vec_pass(source, tile, count, step):
        here = source * row_tiles + tile + BAND
        there = (source - step) * row_tiles + tile + BAND
        return send(win.at[:, :, pl.ds(here, count)], win.at[:, :, pl.ds(there, count)], at_row(step))

    near_parts = []
    if forwarding:
        second = depth_of(2)
        extra = second // 2
        main = row_tiles - extra
        parts = spans(main, 2)
        near_parts.append(vec_send(even * extra + parts[0][0], parts[0][1], sign))
        turned = vec_send(odd * (row_tiles - extra), extra, -2 * sign) if extra else None
    hop_parts = []
    hop_spans = spans(slots, max(1, slots // 12))
    for h, other in enumerate(across):
        for start, count in hop_spans:
            hop_parts.append((ka + 2 * (h + 1), start, count, send(
                hop.at[pl.ds(start, count)], all_hop.at[ka, pl.ds(start, count)], at_ka(other))))
    for other in others:
        send(meta, all_meta.at[ka], at_ka(other))
    if forwarding:
        for start, count in parts[1:]:
            near_parts.append(vec_send(even * extra + start, count, sign))
        if extra:
            vec_send(odd * (row_tiles - extra), extra, sign)
        vec_send(even * (row_tiles - second), second, 2 * sign)
        if second > extra:
            vec_send(even * extra + odd * (row_tiles - second), second - extra, -2 * sign)
    else:
        first = depth_of(1)
        vec_send(0, first, -1)
        vec_send(row_tiles - first, first, 1)
        if reach >= 2:
            vec_send(0, depth_of(2), -2)
            vec_send(row_tiles - depth_of(2), depth_of(2), 2)
    for d in range(3, reach + 1):
        vec_send(0, depth_of(d), -d)
        vec_send(row_tiles - depth_of(d), depth_of(d), d)
    for start, count in hop_spans:
        send(hop.at[pl.ds(start, count)], all_hop.at[ka, pl.ds(start, count)], at_ka(partner))

    fetch_hop.wait()
    fetch_meta.wait()
    store_hop = pltpu.make_async_copy(hop_own, all_hop.at[ka], local_sem.at[0])
    store_meta = pltpu.make_async_copy(meta_own, all_meta.at[ka], local_sem.at[1])
    store_hop.start()
    store_meta.start()

    def pass_hop(n):
        owner, start, count, copy = hop_parts[n]
        owner = lax.rem(owner, group_size)
        arrived(copy)
        block = all_hop.at[owner, pl.ds(start, count)]
        send(block, block, at_ka(partner))

    done = 0
    if forwarding:
        for n, copy in enumerate(near_parts):
            arrived(copy)
            start, count = parts[n]
            vec_pass(sign, odd * extra + start, count, 2 * sign)
            if n == 1 and extra:
                arrived(turned)
                vec_pass(2 * sign, odd * (row_tiles - extra), extra, sign)
            until = len(hop_parts) * (n + 1) // (len(near_parts) + 1)
            while done < until:
                pass_hop(done)
                done += 1
        if len(near_parts) < 2 and extra:
            arrived(turned)
            vec_pass(2 * sign, odd * (row_tiles - extra), extra, sign)
    while done < len(hop_parts):
        pass_hop(done)
        done += 1

    store_hop.wait()
    store_meta.wait()
    for copy in made:
        if id(copy) not in received:
            copy.wait_recv()
    for copy in made:
        copy.wait_send()


def exchange(group_size, row_shards, hop, meta, vec):
    slots = hop.shape[0]
    width = vec.shape[2] + 2 * BAND
    return pl.pallas_call(
        functools.partial(exchange_kernel, group_size, row_shards),
        out_shape=(
            jax.ShapeDtypeStruct((group_size,) + hop.shape, hop.dtype),
            jax.ShapeDtypeStruct((group_size,) + meta.shape, meta.dtype),
            jax.ShapeDtypeStruct(vec.shape[:2] + (width,) + vec.shape[3:], vec.dtype),
        ),
        in_specs=[pl.BlockSpec(memory_space=pl.ANY)] * 3,
        out_specs=(pl.BlockSpec(memory_space=pl.ANY),) * 3,
        scratch_shapes=[
            pltpu.VMEM(hop.shape, hop.dtype),
            pltpu.VMEM(meta.shape, meta.dtype),
            pltpu.SemaphoreType.DMA((96,)),
            pltpu.SemaphoreType.DMA((96,)),
            pltpu.SemaphoreType.DMA((2,)),
        ],
        compiler_params=pltpu.CompilerParams(
            collective_id=0, has_side_effects=True, vmem_limit_bytes=60 * 2**20),
        name="exchange",
    )(hop, meta, vec)


def product_kernel(group_count, order, places, group_rows, coef, hop, vec, win, out,
                   vwin, acc, tiles, mats, tile_sem, vec_sem, out_sem):
    kpoints = vec.shape[0]
    row_tiles = vec.shape[2]
    groups = group_count[0]
    edge = vec.shape[3]

    def tile_copies(g):
        slot = lax.rem(g, DEPTH)
        return [
            pltpu.make_async_copy(hop.at[order[g * GROUP + j]], tiles.at[slot, j], tile_sem.at[slot, j])
            for j in range(GROUP)
        ]

    regions = [
        (win.at[:, :, pl.ds(0, BAND)], vwin.at[:, :, pl.ds(0, BAND)]),
        (vec, vwin.at[:, :, pl.ds(BAND, row_tiles)]),
        (win.at[:, :, pl.ds(BAND + row_tiles, BAND)], vwin.at[:, :, pl.ds(BAND + row_tiles, BAND)]),
    ]
    loads = [pltpu.make_async_copy(s, d, vec_sem.at[n]) for n, (s, d) in enumerate(regions)]
    for copy in loads:
        copy.start()
    for ahead in range(DEPTH - 1):
        @pl.when(ahead < groups)
        def _(ahead=ahead):
            for copy in tile_copies(ahead):
                copy.start()

    def clear(i, _):
        for k in range(kpoints):
            for part in range(2):
                acc[k, part, i] = jnp.zeros(acc.shape[3:], acc.dtype)
        return 0

    lax.fori_loop(0, row_tiles, clear, 0)
    for copy in loads:
        copy.wait()

    def step(g, _):
        @pl.when(g + DEPTH - 1 < groups)
        def _():
            for copy in tile_copies(g + DEPTH - 1):
                copy.start()

        for copy in tile_copies(g):
            copy.wait()
        slot = lax.rem(g, DEPTH)
        target = group_rows[g]
        for k in range(kpoints):
            for j in range(GROUP):
                n = g * GROUP + j
                tile = tiles[slot, j].astype(jnp.float32)
                cosine = (coef[2 * k, n] * tile).astype(jnp.bfloat16)
                sine = coef[2 * k + 1, n] * tile
                left = j * 2 * edge
                mats[k, :edge, left:left + edge] = cosine
                mats[k, edge:, left + edge:left + 2 * edge] = cosine
                mats[k, edge:, left:left + edge] = sine.astype(jnp.bfloat16)
                mats[k, :edge, left + edge:left + 2 * edge] = (-sine).astype(jnp.bfloat16)
        for k in range(kpoints):
            stacked = jnp.concatenate(
                [vwin[k, part, places[g * GROUP + j]] for j in range(GROUP) for part in range(2)],
                axis=0)
            result = jnp.dot(mats[k], stacked, preferred_element_type=jnp.float32)
            for part in range(2):
                acc[k, part, target] += result[part * edge:(part + 1) * edge]
        return 0

    lax.fori_loop(0, groups, step, 0)
    store = pltpu.make_async_copy(acc, out, out_sem)
    store.start()
    store.wait()


def product(group_count, order, places, group_rows, coef, hop, vec, win):
    kpoints, _, row_tiles, edge, vec_count = vec.shape
    smem = pl.BlockSpec(memory_space=pltpu.SMEM)
    return pl.pallas_call(
        product_kernel,
        out_shape=jax.ShapeDtypeStruct(vec.shape, jnp.float32),
        in_specs=[smem] * 5 + [pl.BlockSpec(memory_space=pl.ANY)] * 3,
        out_specs=pl.BlockSpec(memory_space=pl.ANY),
        scratch_shapes=[
            pltpu.VMEM(win.shape, win.dtype),
            pltpu.VMEM(vec.shape, jnp.float32),
            pltpu.VMEM((DEPTH, GROUP, edge, edge), hop.dtype),
            pltpu.VMEM((kpoints, 2 * edge, 2 * GROUP * edge), jnp.bfloat16),
            pltpu.SemaphoreType.DMA((DEPTH, GROUP)),
            pltpu.SemaphoreType.DMA((3,)),
            pltpu.SemaphoreType.DMA,
        ],
        compiler_params=pltpu.CompilerParams(vmem_limit_bytes=60 * 2**20),
        name="product",
    )(group_count, order, places, group_rows, coef, hop, vec, win)


def body(hoppings, tile_rows, tile_cols, tile_lats, tile_counts, phase_angle, vectors):
    edge = hoppings.shape[2]
    per_device = hoppings.shape[1]
    group_size = lax.axis_size("ka")
    row_shards = lax.axis_size("rows")
    kpoints, _, orbitals, vec_count = vectors.shape
    row_tiles = orbitals // edge
    total_tiles = row_tiles * row_shards
    row_start = lax.axis_index("rows") * row_tiles
    slots = group_size * per_device

    lanes = -(-per_device // 128) * 128
    live = lax.broadcasted_iota(jnp.int32, (1, per_device), 1) < tile_counts
    rows = jnp.where(live, tile_rows - row_start, row_tiles)
    place = jnp.mod(tile_cols - row_start + BAND, total_tiles)
    meta = jnp.concatenate([rows, place, tile_lats, jnp.zeros((5, per_device), jnp.int32)], axis=0)
    meta = jnp.pad(meta, ((0, 0), (0, lanes - per_device)))
    vec = vectors.reshape(kpoints, 2, row_tiles, edge, vec_count)
    all_hop, all_meta, win = exchange(group_size, row_shards, hoppings[0], meta, vec)

    all_hop = all_hop.reshape(slots, edge, edge)
    slot_rows = all_meta[:, 0, :per_device].reshape(slots)
    slot_place = all_meta[:, 1, :per_device].reshape(slots)
    slot_lats = all_meta[:, 2, :per_device].reshape(slots)
    group_max = slots // GROUP + row_tiles
    in_row = slot_rows[None, :] == lax.iota(jnp.int32, row_tiles)[:, None]
    row_counts = jnp.sum(in_row.astype(jnp.int32), axis=1)
    row_groups = jnp.maximum((row_counts + GROUP - 1) // GROUP, 1)
    ends = jnp.sum(
        jnp.where(lax.iota(jnp.int32, row_tiles)[None, :] <= lax.iota(jnp.int32, row_tiles)[:, None],
                  row_groups[None, :], 0), axis=1)
    starts = ends - row_groups
    before = lax.iota(jnp.int32, slots)[None, :] < lax.iota(jnp.int32, slots)[:, None]
    same = slot_rows[None, :] == slot_rows[:, None]
    rank = jnp.sum((before & same).astype(jnp.int32), axis=1)
    base = jnp.sum(jnp.where(in_row, starts[:, None], 0), axis=0)
    position = jnp.where(slot_rows < row_tiles, base * GROUP + rank, -1)
    hit = lax.iota(jnp.int32, group_max * GROUP)[:, None] == position[None, :]

    def arranged(values):
        return jnp.sum(jnp.where(hit, values[None, :], 0), axis=1)

    order = arranged(lax.iota(jnp.int32, slots))
    places = arranged(slot_place)
    lats = arranged(slot_lats + 1) - 1
    group_rows = jnp.minimum(
        jnp.sum((lax.iota(jnp.int32, group_max)[:, None] >= ends[None, :]).astype(jnp.int32), axis=1),
        row_tiles - 1)
    weights = jnp.stack([jnp.cos(phase_angle), jnp.sin(phase_angle)], axis=1).reshape(2 * kpoints, -1)
    coef = jnp.sum(
        jnp.where(lats[None, :, None] == lax.iota(jnp.int32, weights.shape[1]), weights[:, None, :], 0.0),
        axis=2)
    out = product(ends[-1:], order, places, group_rows, coef, all_hop, vec, win)
    return out.reshape(kpoints, 2, orbitals, vec_count)


def solution(mesh):
    return jax.shard_map(
        body,
        mesh=mesh,
        in_specs=(
            P("rows", "ka", None, None),
            P("rows", "ka"),
            P("rows", "ka"),
            P("rows", "ka"),
            P("rows", "ka"),
            P("ka", None),
            P("ka", None, "rows", None),
        ),
        out_specs=P("ka", None, "rows", None),
        check_vma=False,
    )
```
